256 devices in a mesh: role: 4 (over x), contr: 16 (over y_lo, z), horiz: 4 (over y_hi, core).
Axes of the slice: x: 4, y: 4 (y_hi: 2, y_lo: 2; y = y_hi * 2 + y_lo), z: 8, core: 2. Of those that a mesh axis runs over, the one named last changes fastest.
Arguments:
- tops: bfloat16 [3, 320, 320, 320], P(None, 'contr', 'horiz', 'role'), may hold values from -6 to 6
- bottoms: bfloat16 [3, 320, 320, 2, 320], P(None, 'contr', 'horiz'), may hold values from -0.01953125 to 0.01953125
- left_iso: bfloat16 [320, 8, 320], P(None, None, 'horiz'), may hold values from -0.3125 to 0.3125
- right_iso: bfloat16 [320, 320, 320], P(('contr', 'horiz')), may hold values from -0.01953125 to 0.01953125
Outputs:
- coarse: float32 [2, 2, 8, 320], replicated
The draws below stay inside these ranges and needn't reach their ends.
All inputs are finite; a program needn't handle non-finite values.
Results may differ from the reference program's by a relative error of at most 0.0081.
Values may be sent and summed in bfloat16 or wider, within the bound.
A program may use at most 128 MiB of HBM per device.

```python
import jax
import jax.numpy as jnp
from jax import lax

CHI = 320
DOWN = 2
A_OUT = 8


def block_levels(own_key, extent, shards, least, largest):
    def one(position, parts):
        heights = jax.random.uniform(jax.random.fold_in(jax.random.fold_in(own_key, 6), position), (parts,), jnp.float32, least / len(shards), largest / len(shards))
        return jnp.repeat(jnp.exp(heights), extent[position] // parts).reshape((-1,) + (1,) * (len(extent) - position - 1))

    gain = one(*shards[0])
    for cut in shards[1:]:
        gain = gain * one(*cut)
    return gain


def bell_draw(stream_key, dims, deviation, most, cuts=(), kind=jnp.bfloat16):
    drawn = deviation * jax.random.normal(stream_key, dims, jnp.float32)
    if cuts:
        drawn = drawn * block_levels(stream_key, dims, cuts, -0.22, 0.18)
    return jnp.clip(drawn, -most, most).astype(kind)


def setup_inputs(seed: int = 0) -> dict:
    seeds = jax.random.split(jax.random.key(seed), 5)
    return {
        "tops": bell_draw(seeds[0], (3, CHI, CHI, CHI), 1.0, 6.0, ((1, 16), (2, 4), (3, 4))),
        "bottoms": bell_draw(seeds[1], (3, CHI, CHI, DOWN, CHI), (CHI * CHI) ** -0.5, 0.01953125, ((1, 16), (2, 4))),
        "left_iso": bell_draw(seeds[2], (CHI, A_OUT, CHI), CHI ** -0.5, 0.3125, ((2, 4),)),
        "right_iso": bell_draw(seeds[3], (CHI, CHI, CHI), (CHI * CHI) ** -0.5, 0.01953125, ((0, 64),)),
    }


def pair_product(top, bottom, left_iso, right_iso):
    count = 8
    width = CHI // count
    top_blocks = jnp.transpose(top.reshape(CHI, count, width, CHI), (1, 0, 2, 3))
    iso_blocks = right_iso.reshape(count, width, CHI, CHI)
    bottom_mat = bottom.reshape(CHI * CHI, DOWN * CHI)
    left_wide = left_iso.astype(jnp.float32)

    def one_block(pieces):
        top_block, iso_block = pieces
        expanded = jnp.einsum('krl,lam->rakm', top_block.astype(jnp.float32), left_wide).astype(jnp.bfloat16)
        summed = jnp.dot(expanded.reshape(width * A_OUT, CHI * CHI), bottom_mat, preferred_element_type=jnp.float32)
        rounded = summed.astype(jnp.bfloat16).reshape(width, A_OUT, DOWN, CHI)
        return jnp.einsum('xadr,xrb->dab', rounded.astype(jnp.float32), iso_block.astype(jnp.float32))

    return jnp.sum(lax.map(one_block, (top_blocks, iso_blocks)), axis=0)


def reference(tops, bottoms, left_iso, right_iso):
    bulk = pair_product(tops[0], bottoms[0], left_iso, right_iso)
    second = pair_product(tops[2], bottoms[0], left_iso, right_iso)
    mixed = pair_product(tops[1], bottoms[1], left_iso, right_iso)
    last = pair_product(tops[0], bottoms[2], left_iso, right_iso)
    moment = 0.25 * second + 0.5 * mixed + 0.25 * last
    return jnp.stack([bulk, moment])
```

```python
import functools

import jax
import jax.numpy as jnp
from jax import lax
from jax.experimental import pallas as pl
from jax.experimental.pallas import tpu as pltpu
from jax.sharding import Mesh
from jax.sharding import PartitionSpec as P

MESH = pl.DeviceIdType.MESH
AXES = ("x", "yl", "z", "yh", "c")
BF = jnp.bfloat16
F32 = jnp.float32

KC = 6
NCH = 3
KT = 2
ROWS = 20
VM = pltpu.VMEM


def place():
    return {a: lax.axis_index(a) for a in AXES}


def at(me, **over):
    return tuple(over.get(a, me[a]) for a in AXES)


def contract_kernel(
    tp, bt, lc, y_out,
    rb, rbt, lhs, lk, xs, xst, bs, bst, acc0, accm, perm,
    t_send, t_recv, f_send, f_recv, b_sem, l_sem,
):
    me = place()
    x, yh, c = me["x"], me["yh"], me["c"]
    barrier = pltpu.get_barrier_semaphore()
    peers = [(dx, dy) for dx in range(4) for dy in range(2) if (dx, dy) != (0, 0)]

    def peer(dx, dy):
        return at(me, x=lax.rem(x + dx, 4), yh=lax.rem(yh + dy, 2))

    partner = at(me, c=1 - c)
    for dx, dy in peers:
        pl.semaphore_signal(barrier, inc=1, device_id=peer(dx, dy), device_id_type=MESH)
    pl.semaphore_signal(barrier, inc=1, device_id=partner, device_id_type=MESH)

    l_copies = []
    for xx in range(4):
        for kind, src, dst, n in ((0, 0, 0, 80), (1, 0, 80, 48), (1, 48, 0, 32), (2, 0, 32, 80)):
            cp = pltpu.make_async_copy(
                lc.at[pl.ds(xx * 80 + src, n), :],
                lk.at[kind, pl.ds(xx * 128 + dst, n), :],
                l_sem.at[len(l_copies)],
            )
            cp.start()
            l_copies.append(cp)
    b_copies = {ch: [] for ch in range(NCH + 1)}
    n = 0
    for ch in range(NCH + 1):
        for kind in range(3):
            for j in range(2 if ch < NCH else 1):
                for d in range(2):
                    if ch < NCH:
                        src = bt.at[kind, d, pl.ds((ch * KC + 3 * j) * 80, 240), :]
                        dst = bs.at[ch, kind, pl.ds(j * 256, 240), pl.ds(d * 384, 384)]
                    else:
                        src = bt.at[kind, d, pl.ds(NCH * KC * 80, 160), :]
                        dst = bst.at[kind, pl.ds(0, 160), pl.ds(d * 384, 384)]
                    cp = pltpu.make_async_copy(src, dst, b_sem.at[n])
                    cp.start()
                    b_copies[ch].append(cp)
                    n += 1
    pl.semaphore_wait(barrier, 8)

    def piece(ch, dx, dy):
        i = dx * 2 + dy
        tx = lax.rem(x + dx, 4)
        h = yh * 2 + c
        if ch is None:
            src = tp.at[tx, pl.ds(NCH * KC * ROWS, KT * ROWS), :]
            dst = rbt.at[h, x]
            s = NCH
        else:
            src = tp.at[tx, pl.ds(pl.multiple_of(ch * (KC * ROWS), 8), KC * ROWS), :]
            dst = rb.at[ch, h, x]
            s = ch
        if (dx, dy) == (0, 0):
            return pltpu.make_async_copy(src, dst, t_recv.at[s, i])
        return pltpu.make_async_remote_copy(
            src, dst, t_send.at[s, i], t_recv.at[s, i], device_id=peer(dx, dy), device_id_type=MESH
        )

    order = [(0, 1), (1, 0), (3, 0), (1, 1), (3, 1), (2, 0), (2, 1), (0, 0)]
    for ch in (0, 1, 2, None):
        for dx, dy in order:
            piece(ch, dx, dy).start()

    for kind, rows in ((0, ((80, 48),)), (1, ((32, 48),)), (2, ((0, 32), (112, 16)))):
        for xx in range(4):
            for r, m in rows:
                lk[kind, xx * 128 + r : xx * 128 + r + m, :] = jnp.zeros((m, 1024), BF)
    for ch in range(NCH):
        for kind in range(3):
            for j in range(2):
                bs[ch, kind, j * 256 + 240 : j * 256 + 256, :] = jnp.zeros((16, 768), BF)
    for kind in range(3):
        bst[kind, 160:256, :] = jnp.zeros((96, 768), BF)
    acc0[...] = jnp.zeros_like(acc0)
    accm[...] = jnp.zeros_like(accm)
    p = lax.broadcasted_iota(jnp.int32, (640, 640), 0)
    q = lax.broadcasted_iota(jnp.int32, (640, 640), 1)
    g = (p * 1639) >> 16
    rest = p - g * 40
    src_row = (rest & 7) * 80 + g * 5 + (rest >> 3)
    perm[...] = jnp.where(src_row == q, 1.0, 0.0).astype(BF)
    for cp in l_copies:
        cp.wait()

    def forward(ch, s, dy):
        h = dy * 2 + c
        ref = rbt.at[h] if ch is None else rb.at[ch, h]
        return pltpu.make_async_remote_copy(
            ref, ref, f_send.at[s, dy], f_recv.at[s, dy], device_id=partner, device_id_type=MESH
        )

    def arrive(ch, s):
        for dx in range(4):
            for dy in range(2):
                cp = piece(ch, dx, dy)
                if (dx, dy) == (0, 0):
                    cp.wait()
                else:
                    cp.wait_recv()
        for dy in range(2):
            forward(ch, s, dy).start()

    def arrived(ch, s):
        for dy in range(2):
            forward(ch, s, dy).wait_recv()

    lane = lax.broadcasted_iota(jnp.int32, (ROWS, 128), 1)
    low = lane < 64
    lane80 = lax.broadcasted_iota(jnp.int32, (80, 128), 1)

    def expand(buf, kc, out, width):
        for kk in range(kc):
            for h in range(4):
                for xx in range(4):
                    t0 = buf[h, xx, kk * ROWS : (kk + 1) * ROWS, 0:128]
                    t1 = buf[h, xx, kk * ROWS : (kk + 1) * ROWS, 128:256]
                    rows = slice(kk * 80 + h * ROWS, kk * 80 + (h + 1) * ROWS)
                    cols = slice(xx * 128, xx * 128 + 128)
                    lhs[0, rows, cols] = t0
                    lhs[1, rows, cols] = jnp.where(low, t1, t0)
                    lhs[2, rows, cols] = t1
        for kind in range(3):
            xv = jnp.dot(lhs[kind, 0 : kc * 80, :], lk[kind], preferred_element_type=F32)
            if kind == 1:
                xv = xv * 2.0
            base = (2 - kind) * width
            for j in range((kc + 2) // 3):
                for a in range(8):
                    def part(s):
                        k = 3 * j + s
                        return xv[k * 80 : (k + 1) * 80, a * 128 : (a + 1) * 128]
                    mid = pltpu.roll(part(1), 80, 1)
                    first = jnp.where(lane80 < 80, part(0), mid)
                    if 3 * j + 2 < kc:
                        last = pltpu.roll(part(2), 32, 1)
                    else:
                        last = jnp.zeros((80, 128), F32)
                    second = jnp.where(lane80 < 32, mid, last)
                    col = base + j * 256
                    out[a * 80 : (a + 1) * 80, col : col + 128] = first.astype(BF)
                    out[a * 80 : (a + 1) * 80, col + 128 : col + 256] = second.astype(BF)

    arrive(0, 0)

    def step(ch, carry):
        arrived(ch, ch)
        expand(rb.at[ch], KC, xs, 512)
        for i in range(12):
            b_wait(ch, i)
        accm[...] += jnp.dot(xs[...], bs[ch].reshape(1536, 768), preferred_element_type=F32)

        @pl.when(ch < NCH - 1)
        def _():
            arrive(ch + 1, ch + 1)

        @pl.when(ch == NCH - 1)
        def _():
            arrive(None, NCH)

        acc0[...] += jnp.dot(xs[:, 1024:1536], bs[ch, 0], preferred_element_type=F32)
        return carry

    def b_wait(ch, i):
        pltpu.make_async_copy(
            bt.at[0, 0, pl.ds(0, 240), :], bs.at[0, 0, pl.ds(0, 240), pl.ds(0, 384)], b_sem.at[ch * 12 + i]
        ).wait()

    lax.fori_loop(0, NCH, step, 0)
    arrived(None, NCH)
    expand(rbt, KT, xst, 256)
    for cp in b_copies[NCH]:
        cp.wait()
    accm[...] += jnp.dot(xst[...], bst[...].reshape(768, 768), preferred_element_type=F32)
    acc0[...] += jnp.dot(xst[:, 512:768], bst[0], preferred_element_type=F32)

    for i, acc in enumerate((acc0, accm)):
        mixed = acc[:, 256:384] + pltpu.roll(acc[:, 640:768], 64, 1)
        packed = jnp.concatenate(
            [acc[:, 0:256].astype(BF), acc[:, 384:640].astype(BF), mixed.astype(BF)], axis=1
        )
        moved = jnp.dot(perm[...], packed, preferred_element_type=F32)
        y_out[i] = moved.reshape(16, 40, 640).astype(BF)

    for ch in (0, 1, 2, None):
        s = NCH if ch is None else ch
        for dx, dy in peers:
            piece(ch, dx, dy).wait_send()
        for dy in range(2):
            forward(ch, s, dy).wait_send()


def contract(tp, bt, lc):
    any_space = pl.BlockSpec(memory_space=pl.ANY)
    return pl.pallas_call(
        contract_kernel,
        out_shape=jax.ShapeDtypeStruct((2, 16, 40, 640), BF),
        in_specs=[any_space] * 3,
        out_specs=pl.BlockSpec(memory_space=VM),
        scratch_shapes=[
            VM((NCH, 4, 4, KC * ROWS, 256), BF),
            VM((4, 4, KT * ROWS, 256), BF),
            VM((3, KC * 80, 512), BF),
            VM((3, 512, 1024), BF),
            VM((640, 1536), BF),
            VM((640, 768), BF),
            VM((NCH, 3, 512, 768), BF),
            VM((3, 256, 768), BF),
            VM((640, 768), F32),
            VM((640, 768), F32),
            VM((640, 640), BF),
            pltpu.SemaphoreType.DMA((NCH + 1, 8)),
            pltpu.SemaphoreType.DMA((NCH + 1, 8)),
            pltpu.SemaphoreType.DMA((NCH + 1, 2)),
            pltpu.SemaphoreType.DMA((NCH + 1, 2)),
            pltpu.SemaphoreType.DMA((42,)),
            pltpu.SemaphoreType.DMA((16,)),
        ],
        compiler_params=pltpu.CompilerParams(
            collective_id=0, has_side_effects=True, vmem_limit_bytes=60 << 20
        ),
    )(tp, bt, lc)


def reduce_kernel(
    y_in, r_in, out,
    swap, work, up_s, up_r, dn_s, dn_r, part, parts, rk, pz, pzs, py, pys, px,
    c_sem, up_sem, dn_sem, s_sem, r_sem, z_sem, y_sem, x_sem,
):
    me = place()
    x, yl, z, yh, c = (me[a] for a in AXES)
    barrier = pltpu.get_barrier_semaphore()

    def to_z(k):
        return at(me, z=lax.rem(z + k, 8))

    def to_yc(k):
        mine = yl * 4 + yh * 2 + c
        v = lax.rem(mine + k, 8)
        return at(me, yl=v // 4, yh=lax.rem(v // 2, 2), c=lax.rem(v, 2))

    def to_x(k):
        return at(me, x=lax.rem(x + k, 4))

    own_role = yh * 2 + c
    for k in range(1, 8):
        pl.semaphore_signal(barrier, inc=1, device_id=to_z(k), device_id_type=MESH)
        pl.semaphore_signal(barrier, inc=1, device_id=to_yc(k), device_id_type=MESH)
    for k in range(1, 4):
        pl.semaphore_signal(barrier, inc=1, device_id=to_x(k), device_id_type=MESH)
    for sl in range(2):
        for sh in range(2):
            same = (own_role == x) & (sl == yl) & (sh == yh) & (lax.rem(x, 2) == c)

            @pl.when(jnp.logical_not(same))
            def _():
                pl.semaphore_signal(
                    barrier, inc=1, device_id=at(me, x=own_role, yl=sl, yh=sh, c=lax.rem(x, 2)),
                    device_id_type=MESH,
                )

    def target(tl, d):
        return d * 2 + c, tl, x // 2, lax.rem(x, 2)

    def is_self(tl, d):
        tx, tyl, tyh, tc = target(tl, d)
        return (tx == x) & (tyl == yl) & (tyh == yh) & (tc == c)

    selfs = [jnp.where(is_self(tl, d), 1, 0) for tl in range(2) for d in range(2)]
    pl.semaphore_wait(barrier, 17 + 4 - (selfs[0] + selfs[1] + selfs[2] + selfs[3]))

    partner = at(me, c=1 - c)
    sw = pltpu.make_async_remote_copy(
        y_in.at[1 - c], swap, c_sem.at[0], c_sem.at[1], device_id=partner, device_id_type=MESH
    )
    sw.start()
    r_copies = []
    for t in range(5):
        for i, (src, dst, n) in enumerate(((0, 0, 320), (256, 320, 64))):
            cp = pltpu.make_async_copy(
                r_in.at[t, pl.ds(src, n), :], rk.at[t, pl.ds(dst, n), :], r_sem.at[t * 2 + i]
            )
            cp.start()
            r_copies.append(cp)
    sw.wait()
    work[...] = (y_in[c].astype(F32) + swap[...].astype(F32)).astype(BF)

    def up(g, s):
        src = up_s.at[g, s]
        return pltpu.make_async_remote_copy(
            src, up_r.at[g, s], up_sem.at[0, g, s], up_sem.at[1, g, s],
            device_id=at(me, z=lax.rem(z + 1, 8)), device_id_type=MESH,
        )

    def dn(g, s):
        return pltpu.make_async_remote_copy(
            dn_s.at[g, s], dn_r.at[g, s], dn_sem.at[0, g, s], dn_sem.at[1, g, s],
            device_id=at(me, z=lax.rem(z + 7, 8)), device_id_type=MESH,
        )

    for s in range(4):
        for g in range(2):
            mine = work[g * 8 + lax.rem(z - (4 - s) + 8, 8)]
            if s > 0:
                dn(g, s - 1).wait_recv()
                mine = (mine.astype(F32) + dn_r[g, s - 1].astype(F32)).astype(BF)
            dn_s[g, s] = mine
            dn(g, s).start()
            if s < 3:
                mine = work[g * 8 + lax.rem(z + (3 - s), 8)]
                if s > 0:
                    up(g, s - 1).wait_recv()
                    mine = (mine.astype(F32) + up_r[g, s - 1].astype(F32)).astype(BF)
                up_s[g, s] = mine
                up(g, s).start()
    slot = yl * 2 + yh
    for g in range(2):
        up(g, 2).wait_recv()
        dn(g, 3).wait_recv()
        total = (
            work[g * 8 + z].astype(F32) + up_r[g, 2].astype(F32) + dn_r[g, 3].astype(F32)
        ).astype(BF)
        for d in range(2):
            part[g, d, :, 0:256] = total[:, d * 256 : d * 256 + 256]
            part[g, d, :, 256:384] = total[:, 512:640]

    def scatter(tl, d):
        tx, tyl, tyh, tc = target(tl, d)
        return pltpu.make_async_remote_copy(
            part.at[tl, d], parts.at[slot], s_sem.at[0, tl * 2 + d], s_sem.at[1, slot],
            device_id=(tx, tyl, z, tyh, tc), device_id_type=MESH,
        )

    def keep(tl, d):
        return pltpu.make_async_copy(part.at[tl, d], parts.at[slot], s_sem.at[1, slot])

    for tl in range(2):
        for d in range(2):
            @pl.when(jnp.logical_not(is_self(tl, d)))
            def _():
                scatter(tl, d).start()

            @pl.when(is_self(tl, d))
            def _():
                keep(tl, d).start()
    for i in range(4):
        pltpu.make_async_copy(part.at[0, 0], parts.at[i], s_sem.at[1, i]).wait()
    whole = (
        parts[0].astype(F32) + parts[1].astype(F32) + parts[2].astype(F32) + parts[3].astype(F32)
    )
    lanes = lax.broadcasted_iota(jnp.int32, (40, 384), 1)
    d_here = x // 2
    keep_lane = (lanes < 256) | ((lanes < 320) == (d_here == 0))
    whole = jnp.where(keep_lane, whole, 0.0)
    for cp in r_copies:
        cp.wait()
    total = jnp.zeros((8, 320), F32)
    for t in range(5):
        total += jnp.dot(
            whole[t * 8 : t * 8 + 8, :].astype(BF), rk[t], preferred_element_type=F32
        )
    pzs[...] = total

    def all_sum(src, land, sem, n, dest):
        copies = []
        for k in range(1, n):
            cp = pltpu.make_async_remote_copy(
                src, land.at[k], sem.at[0, k], sem.at[1, k], device_id=dest(k), device_id_type=MESH
            )
            cp.start()
            copies.append(cp)
        for cp in copies:
            cp.wait()
        s = src[...]
        for k in range(1, n):
            s = s + land[k]
        return s

    pys[...] = all_sum(pzs, pz, z_sem, 8, to_z)
    own = all_sum(pys, py, y_sem, 8, to_yc)
    scale = jnp.where(lax.rem(x, 2) == 0, 1.0, 0.25)
    px[x] = own * scale
    copies = []
    for k in range(1, 4):
        cp = pltpu.make_async_remote_copy(
            px.at[x], px.at[x], x_sem.at[0, k], x_sem.at[1, k], device_id=to_x(k), device_id_type=MESH
        )
        cp.start()
        copies.append(cp)
    for cp in copies:
        cp.wait()
    for i in range(4):
        out[i % 2, i // 2] = px[i]

    sw_done = [(g, s) for g in range(2) for s in range(4)]
    for g, s in sw_done:
        dn(g, s).wait_send()
        if s < 3:
            up(g, s).wait_send()
    for tl in range(2):
        for d in range(2):
            @pl.when(jnp.logical_not(is_self(tl, d)))
            def _():
                scatter(tl, d).wait_send()


def reduce_all(y, r):
    return pl.pallas_call(
        reduce_kernel,
        out_shape=jax.ShapeDtypeStruct((2, 2, 8, 320), F32),
        in_specs=[pl.BlockSpec(memory_space=VM), pl.BlockSpec(memory_space=pl.ANY)],
        out_specs=pl.BlockSpec(memory_space=VM),
        scratch_shapes=[
            VM((16, 40, 640), BF),
            VM((16, 40, 640), BF),
            VM((2, 3, 40, 640), BF),
            VM((2, 3, 40, 640), BF),
            VM((2, 4, 40, 640), BF),
            VM((2, 4, 40, 640), BF),
            VM((2, 2, 40, 384), BF),
            VM((4, 40, 384), BF),
            VM((5, 384, 320), BF),
            VM((8, 8, 320), F32),
            VM((8, 320), F32),
            VM((8, 8, 320), F32),
            VM((8, 320), F32),
            VM((4, 8, 320), F32),
            pltpu.SemaphoreType.DMA((2,)),
            pltpu.SemaphoreType.DMA((2, 2, 3)),
            pltpu.SemaphoreType.DMA((2, 2, 4)),
            pltpu.SemaphoreType.DMA((2, 4)),
            pltpu.SemaphoreType.DMA((10,)),
            pltpu.SemaphoreType.DMA((2, 8)),
            pltpu.SemaphoreType.DMA((2, 8)),
            pltpu.SemaphoreType.DMA((2, 4)),
        ],
        compiler_params=pltpu.CompilerParams(
            collective_id=1, has_side_effects=True, vmem_limit_bytes=60 << 20
        ),
    )(y, r)


def prepare(tops, bottoms, left_iso):
    t = tops.reshape(3, 20, 4, 4, 5, 80)
    t = jnp.transpose(t, (3, 1, 2, 4, 0, 5)).reshape(4, 400, 240)
    tp = jnp.pad(t, ((0, 0), (0, 0), (0, 16)))
    b = jnp.transpose(bottoms, (0, 3, 1, 2, 4)).reshape(3, 2, 1600, 320)
    bt = jnp.pad(b, ((0, 0), (0, 0), (0, 0), (0, 64)))
    lc = jnp.pad(left_iso, ((0, 0), (0, 0), (0, 48))).reshape(320, 1024)
    return tp, bt, lc


def on_device(tops, bottoms, left_iso, right_iso):
    y = contract(*prepare(tops, bottoms, left_iso))
    return reduce_all(y, right_iso)


def solution(mesh):
    torus = Mesh(mesh.devices.reshape(4, 2, 8, 2, 2), AXES)
    in_specs = (
        P(None, ("yl", "z"), ("yh", "c"), "x"),
        P(None, ("yl", "z"), ("yh", "c"), None, None),
        P(None, None, ("yh", "c")),
        P(("yl", "z", "yh", "c"), None, None),
    )
    return jax.shard_map(on_device, mesh=torus, in_specs=in_specs, out_specs=P(), check_vma=False)
```

```python
import jax
import jax.numpy as jnp
from jax import lax
from jax.experimental import pallas as pl
from jax.experimental.pallas import tpu as pltpu
from jax.sharding import Mesh
from jax.sharding import PartitionSpec as P

MESH = pl.DeviceIdType.MESH
AXES = ("x", "yl", "z", "yh", "c")
BF = jnp.bfloat16
F32 = jnp.float32
VM = pltpu.VMEM
DMA = pltpu.SemaphoreType.DMA

ROWS = 20
KINDS = (0, 2, 1)
PARTNER = {0: 1, 1: 2, 2: 0}
NCH = 5
CR = 80
DEEP = 1024


def kernel(
    t_in, b_in, l_in, r_in, out,
    tbuf, tp, rb, bbuf, bm, b0, lhs, lk, xs, acc0, accm, perm,
    give, swap, work, land, up_s, up_r, dn_s, dn_r, part, parts, rk, pz, pzs, py, pys, px,
    t_send, t_recv, f_send, f_recv, b_sem, r_sem,
    c_sem, d_sem, up_sem, dn_sem, s_sem, z_sem, y_sem, x_sem,
):
    x, yl, z, yh, c = (lax.axis_index(a) for a in AXES)
    me = {"x": x, "yl": yl, "z": z, "yh": yh, "c": c}

    def at(**over):
        return tuple(over.get(a, me[a]) for a in AXES)

    def near(dx, dy):
        return at(x=lax.rem(x + dx, 4), yh=lax.rem(yh + dy, 2))

    def to_z(k):
        return at(z=lax.rem(z + k, 8))

    def to_yc(k):
        v = lax.rem(yl * 4 + yh * 2 + c + k, 8)
        return at(yl=v // 4, yh=lax.rem(v // 2, 2), c=lax.rem(v, 2))

    def to_x(k):
        return at(x=lax.rem(x + k, 4))

    partner = at(c=1 - c)
    barrier = pltpu.get_barrier_semaphore()

    def greet(device):
        pl.semaphore_signal(barrier, inc=1, device_id=device, device_id_type=MESH)

    t_copy = pltpu.make_async_copy(t_in, tbuf, b_sem.at[3])
    t_copy.start()
    b_copies = [pltpu.make_async_copy(b_in.at[k], bbuf.at[k], b_sem.at[k]) for k in range(3)]
    for k in KINDS:
        b_copies[k].start()

    peers = [(dx, dy) for dx in range(4) for dy in range(2) if (dx, dy) != (0, 0)]
    for k in range(1, 8):
        greet(to_z(k))
    for dx, dy in peers:
        greet(near(dx, dy))
    for k in range(1, 8):
        greet(to_yc(k))
    own_role = yh * 2 + c
    for sl in range(2):
        for sh in range(2):
            same = (own_role == x) & (x // 2 == c) & (sl == yl) & (sh == yh)

            @pl.when(jnp.logical_not(same))
            def _():
                greet(at(x=own_role, yl=sl, yh=sh, c=x // 2))

    def is_self(q, g):
        return (c * 2 + q == x) & (g == yl) & (x // 2 == yh) & (lax.rem(x, 2) == c)

    n_self = 0
    for q in range(2):
        for g in range(2):
            n_self = n_self + jnp.where(is_self(q, g), 1, 0)

    p = lax.broadcasted_iota(jnp.int32, (80, 80), 0)
    q_ = lax.broadcasted_iota(jnp.int32, (80, 80), 1)
    jj = (p * 3277) >> 16
    rest = p - jj * 20
    cc = (rest * 13108) >> 16
    group = jnp.where(cc * 20 + jj * 5 + (rest - cc * 5) == q_, 1.0, 0.0).astype(BF)
    lane80 = lax.broadcasted_iota(jnp.int32, (80, 128), 1)
    tail = jnp.zeros((80, 48), F32)

    def turned(block, s):
        block = jnp.concatenate([block.astype(F32), tail], axis=1)
        return block if s == 0 else pltpu.roll(block, (0, 80, 32)[s], 1)

    t_copy.wait()
    def top(kk):
        return tbuf[KINDS[kk // 20], kk % 20]

    for j in range(20):
        mid = turned(top(3 * j + 1), 1)
        packed = jnp.concatenate(
            [
                jnp.where(lane80 < 80, turned(top(3 * j), 0), mid).astype(BF),
                jnp.where(lane80 < 32, mid, turned(top(3 * j + 2), 2)).astype(BF),
            ],
            axis=1,
        )
        moved = jnp.dot(group, packed, preferred_element_type=F32).astype(BF)
        for to in range(4):
            tp[to, j * ROWS : (j + 1) * ROWS, :] = moved[to * ROWS : (to + 1) * ROWS, :]
    pl.semaphore_wait(barrier, 25 - n_self)

    def rows_of(n):
        return pl.ds(n * CR, CR)

    def piece(n, dx, dy):
        i = dx * 2 + dy
        src = tp.at[lax.rem(x + dx, 4), rows_of(n), :]
        dst = rb.at[yh * 2 + c, x, rows_of(n), :]
        if (dx, dy) == (0, 0):
            return pltpu.make_async_copy(src, dst, t_recv.at[n, i])
        return pltpu.make_async_remote_copy(
            src, dst, t_send.at[n, i], t_recv.at[n, i], device_id=near(dx, dy), device_id_type=MESH
        )

    order = [(0, 1), (1, 0), (3, 0), (1, 1), (3, 1), (2, 0), (2, 1), (0, 0)]
    for n in range(NCH):
        for dx, dy in order:
            piece(n, dx, dy).start()

    d_here = x // 2
    r_copies = []
    for t in range(5):
        for i, (src, dst, n) in enumerate(
            ((0, d_here * 128, 256), (256, 256 - d_here * 192, 64), (256, 320 - d_here * 320, 64))
        ):
            cp = pltpu.make_async_copy(
                r_in.at[t, pl.ds(src, n), :],
                rk.at[t, pl.ds(pl.multiple_of(dst, 64), n), :],
                r_sem.at[t * 3 + i],
            )
            cp.start()
            r_copies.append(cp)

    for a in range(8):
        row = l_in[a]
        for xx in range(4):
            block = row[:, xx * 80 : xx * 80 + 80]
            for s in range(3):
                lk[s, a * 128 : a * 128 + 80, xx * 128 : xx * 128 + 128] = turned(block, s).astype(BF)
        for s in range(3):
            lk[s, a * 128 + 80 : a * 128 + 128, :] = jnp.zeros((48, 512), BF)
    p = lax.broadcasted_iota(jnp.int32, (640, 640), 0)
    q_ = lax.broadcasted_iota(jnp.int32, (640, 640), 1)
    g_ = (p * 1639) >> 16
    rest = p - g_ * 40
    perm[...] = jnp.where((rest & 7) * 80 + g_ * 5 + (rest >> 3) == q_, 1.0, 0.0).astype(BF)
    for j in range(20):
        bm[j * 256 + 240 : j * 256 + 256, :] = jnp.zeros((16, 640), BF)
    for j in range(7):
        r = 240 if j < 6 else 160
        b0[j * 256 + r : j * 256 + 256, :] = jnp.zeros((256 - r, 640), BF)

    def bottoms(kind):
        b_copies[kind].wait()

        def row_of(kk):
            return pl.ds(pl.multiple_of((kk // 3) * 256 + lax.rem(kk, 3) * 80, 16), 80)

        def turn(k, carry):
            w = jnp.swapaxes(bbuf[kind, k], 0, 1)
            cat = jnp.concatenate([w[0], w[1][:, 256:320], w[1][:, 0:256]], axis=1)
            if kind == 0:
                b0[row_of(k), :] = cat
            bm[row_of(k + 20 * PARTNER[kind]), :] = cat * 2 if kind == 1 else cat
            return carry

        lax.fori_loop(0, 20, turn, 0)

    def forward(n, dy):
        ref = rb.at[dy * 2 + c, :, rows_of(n), :]
        return pltpu.make_async_remote_copy(
            ref, ref, f_send.at[n, dy], f_recv.at[n, dy], device_id=partner, device_id_type=MESH
        )

    def arrive(n):
        for dx in range(4):
            for dy in range(2):
                cp = piece(n, dx, dy)
                if (dx, dy) == (0, 0):
                    cp.wait()
                else:
                    cp.wait_recv()
        for dy in range(2):
            forward(n, dy).start()

    low = lax.broadcasted_iota(jnp.int32, (ROWS, 128), 1) < 64

    def expand(n):
        for dy in range(2):
            forward(n, dy).wait_recv()
        for j in range(4):
            src = slice((n * 4 + j) * ROWS, (n * 4 + j + 1) * ROWS)
            for h in range(4):
                rows = slice(j * 80 + h * ROWS, j * 80 + (h + 1) * ROWS)
                for xx in range(4):
                    t0 = rb[h, xx, src, 0:128]
                    t1 = rb[h, xx, src, 128:256]
                    cols = slice(xx * 128, xx * 128 + 128)
                    lhs[0, rows, cols] = t0
                    lhs[1, rows, cols] = jnp.where(low, t1, t0)
                    lhs[2, rows, cols] = t1
        xv = []
        for s in range(3):
            xv.append(
                lax.dot_general(lhs[s], lk[s], (((1,), (1,)), ((), ())), preferred_element_type=F32)
            )
        for j in range(4):
            for a in range(8):
                box = (slice(j * 80, j * 80 + 80), slice(a * 128, a * 128 + 128))
                mid = pltpu.roll(xv[1][box], 80, 1)
                last = pltpu.roll(xv[2][box], 32, 1)
                rows = slice(a * 80, a * 80 + 80)
                xs[rows, j * 256 : j * 256 + 128] = jnp.where(lane80 < 80, xv[0][box], mid).astype(BF)
                xs[rows, j * 256 + 128 : j * 256 + 256] = jnp.where(lane80 < 32, mid, last).astype(BF)

    def mixed(n):
        return jnp.dot(xs[...], bm[n * DEEP : (n + 1) * DEEP, :], preferred_element_type=F32)

    def window(d):
        return pl.ds(pl.multiple_of(d * 256, 256), 384)

    def swap_copy(q):
        return pltpu.make_async_remote_copy(
            give.at[q], swap.at[q], c_sem.at[0, q], c_sem.at[1, q],
            device_id=partner, device_id_type=MESH,
        )

    def share(q, acc):
        give[q] = acc[:, window(1 - c)].astype(BF)
        swap_copy(q).start()

    def shared(q, acc):
        swap_copy(q).wait_recv()
        mine = (acc[:, window(c)] + swap[q].astype(F32)).astype(BF)
        moved = jnp.dot(perm[...], mine, preferred_element_type=F32)
        work[q] = moved.reshape(2, 8, 40, 384).astype(BF)

    def direct(k):
        return pltpu.make_async_remote_copy(
            work.at[0, :, lax.rem(z + k, 8)], land.at[k], d_sem.at[0, k], d_sem.at[1, k],
            device_id=to_z(k), device_id_type=MESH,
        )

    def up(g, s):
        return pltpu.make_async_remote_copy(
            up_s.at[g, s], up_r.at[g, s], up_sem.at[0, g, s], up_sem.at[1, g, s],
            device_id=to_z(1), device_id_type=MESH,
        )

    def dn(g, s):
        return pltpu.make_async_remote_copy(
            dn_s.at[g, s], dn_r.at[g, s], dn_sem.at[0, g, s], dn_sem.at[1, g, s],
            device_id=to_z(7), device_id_type=MESH,
        )

    slot = yl * 2 + yh

    def scatter(q, g):
        return pltpu.make_async_remote_copy(
            part.at[q, g], parts.at[slot], s_sem.at[0, q * 2 + g], s_sem.at[1, slot],
            device_id=(c * 2 + q, g, z, x // 2, lax.rem(x, 2)), device_id_type=MESH,
        )

    def hand_on(q, g, total):
        part[q, g] = total.astype(BF)

        @pl.when(jnp.logical_not(is_self(q, g)))
        def _():
            scatter(q, g).start()

        @pl.when(is_self(q, g))
        def _():
            pltpu.make_async_copy(part.at[q, g], parts.at[slot], s_sem.at[1, slot]).start()

    def gathered():
        for k in range(1, 8):
            direct(k).wait_recv()
        for g in range(2):
            total = work[0, g, z].astype(F32)
            for k in range(1, 8):
                total = total + land[k, g].astype(F32)
            hand_on(0, g, total)

    def ring():
        for s in range(4):
            for g in range(2):
                mine = work[1, g, lax.rem(z + 4 + s, 8)]
                if s > 0:
                    dn(g, s - 1).wait_recv()
                    mine = (mine.astype(F32) + dn_r[g, s - 1].astype(F32)).astype(BF)
                dn_s[g, s] = mine
                dn(g, s).start()
                if s < 3:
                    mine = work[1, g, lax.rem(z + 3 - s, 8)]
                    if s > 0:
                        up(g, s - 1).wait_recv()
                        mine = (mine.astype(F32) + up_r[g, s - 1].astype(F32)).astype(BF)
                    up_s[g, s] = mine
                    up(g, s).start()
        for g in range(2):
            up(g, 2).wait_recv()
            dn(g, 3).wait_recv()
            hand_on(
                1, g,
                work[1, g, z].astype(F32) + up_r[g, 2].astype(F32) + dn_r[g, 3].astype(F32),
            )

    bottoms(0)
    arrive(0)
    expand(0)
    arrive(1)
    acc0[...] = jnp.dot(xs[...], b0[0:DEEP, :], preferred_element_type=F32)
    bottoms(2)
    accm[...] = mixed(0)
    expand(1)
    arrive(2)
    acc0[...] += jnp.dot(xs[:, 0:768], b0[DEEP:1792, :], preferred_element_type=F32)
    share(0, acc0)
    accm[...] += mixed(1)
    shared(0, acc0)
    for k in (4, 3, 5, 2, 6, 1, 7):
        direct(k).start()
    expand(2)
    bottoms(1)
    arrive(3)
    accm[...] += mixed(2)
    expand(3)
    arrive(4)
    accm[...] += mixed(3)
    expand(4)
    accm[...] += mixed(4)
    share(1, accm)
    gathered()
    shared(1, accm)
    ring()

    for i in range(4):
        pltpu.make_async_copy(part.at[0, 0], parts.at[i], s_sem.at[1, i]).wait()
    whole = (
        parts[0].astype(F32) + parts[1].astype(F32) + parts[2].astype(F32) + parts[3].astype(F32)
    )
    lanes = lax.broadcasted_iota(jnp.int32, (40, 384), 1) + d_here * 1024
    whole = jnp.where((lanes < 320) | (lanes >= 1088), whole, 0.0)
    for cp in r_copies:
        cp.wait()
    total = jnp.zeros((8, 320), F32)
    for t in range(5):
        total += jnp.dot(
            whole[t * 8 : t * 8 + 8, :].astype(BF), rk[t], preferred_element_type=F32
        )
    pzs[...] = total

    def all_sum(src, land, sem, n, dest):
        copies = []
        for k in range(1, n):
            cp = pltpu.make_async_remote_copy(
                src, land.at[k], sem.at[0, k], sem.at[1, k], device_id=dest(k), device_id_type=MESH
            )
            cp.start()
            copies.append(cp)
        for cp in copies:
            cp.wait()
        s = src[...]
        for k in range(1, n):
            s = s + land[k]
        return s

    pys[...] = all_sum(pzs, pz, z_sem, 8, to_z)
    own = all_sum(pys, py, y_sem, 8, to_yc)
    px[x] = own * jnp.where(lax.rem(x, 2) == 0, 1.0, 0.25)
    copies = []
    for k in range(1, 4):
        cp = pltpu.make_async_remote_copy(
            px.at[x], px.at[x], x_sem.at[0, k], x_sem.at[1, k], device_id=to_x(k), device_id_type=MESH
        )
        cp.start()
        copies.append(cp)
    for cp in copies:
        cp.wait()
    for i in range(4):
        out[i % 2, i // 2] = px[i]

    for n in range(NCH):
        for dx, dy in peers:
            piece(n, dx, dy).wait_send()
        for dy in range(2):
            forward(n, dy).wait_send()
    for k in range(1, 8):
        direct(k).wait_send()
    for q in range(2):
        swap_copy(q).wait_send()
        for s in range(4):
            dn(q, s).wait_send()
            if s < 3:
                up(q, s).wait_send()
        for g in range(2):
            @pl.when(jnp.logical_not(is_self(q, g)))
            def _():
                scatter(q, g).wait_send()


def on_device(tops, bottoms, left_iso, right_iso):
    any_space = pl.BlockSpec(memory_space=pl.ANY)
    vmem_space = pl.BlockSpec(memory_space=VM)
    return pl.pallas_call(
        kernel,
        out_shape=jax.ShapeDtypeStruct((2, 2, 8, 320), F32),
        in_specs=[any_space, any_space, vmem_space, any_space],
        out_specs=vmem_space,
        scratch_shapes=[
            VM((3, 20, 80, 80), BF),
            VM((4, 400, 256), BF),
            VM((4, 4, 400, 256), BF),
            VM((3, 20, 80, 2, 320), BF),
            VM((5120, 640), BF),
            VM((1792, 640), BF),
            VM((3, 320, 512), BF),
            VM((3, 1024, 512), BF),
            VM((640, DEEP), BF),
            VM((640, 640), F32),
            VM((640, 640), F32),
            VM((640, 640), BF),
            VM((2, 640, 384), BF),
            VM((2, 640, 384), BF),
            VM((2, 2, 8, 40, 384), BF),
            VM((8, 2, 40, 384), BF),
            VM((2, 3, 40, 384), BF),
            VM((2, 3, 40, 384), BF),
            VM((2, 4, 40, 384), BF),
            VM((2, 4, 40, 384), BF),
            VM((2, 2, 40, 384), BF),
            VM((4, 40, 384), BF),
            VM((5, 384, 320), BF),
            VM((8, 8, 320), F32),
            VM((8, 320), F32),
            VM((8, 8, 320), F32),
            VM((8, 320), F32),
            VM((4, 8, 320), F32),
            DMA((NCH, 8)),
            DMA((NCH, 8)),
            DMA((NCH, 2)),
            DMA((NCH, 2)),
            DMA((4,)),
            DMA((15,)),
            DMA((2, 2)),
            DMA((2, 8)),
            DMA((2, 2, 3)),
            DMA((2, 2, 4)),
            DMA((2, 4)),
            DMA((2, 8)),
            DMA((2, 8)),
            DMA((2, 4)),
        ],
        compiler_params=pltpu.CompilerParams(
            collective_id=0, has_side_effects=True, vmem_limit_bytes=60 << 20
        ),
    )(tops, bottoms, jnp.transpose(left_iso, (1, 2, 0)), right_iso)


def solution(mesh):
    torus = Mesh(mesh.devices.reshape(4, 2, 8, 2, 2), AXES)
    in_specs = (
        P(None, ("yl", "z"), ("yh", "c"), "x"),
        P(None, ("yl", "z"), ("yh", "c"), None, None),
        P(None, None, ("yh", "c")),
        P(("yl", "z", "yh", "c"), None, None),
    )
    return jax.shard_map(on_device, mesh=torus, in_specs=in_specs, out_specs=P(), check_vma=False)
```

```python
import jax
import jax.numpy as jnp
from jax import lax
from jax.experimental import pallas as pl
from jax.experimental.pallas import tpu as pltpu
from jax.sharding import Mesh
from jax.sharding import PartitionSpec as P

MESH = pl.DeviceIdType.MESH
AXES = ("x", "yl", "z", "yh", "c")
BF = jnp.bfloat16
F32 = jnp.float32
VM = pltpu.VMEM
DMA = pltpu.SemaphoreType.DMA

ROWS = 20
KINDS = (0, 2, 1)
PARTNER = {0: 1, 1: 2, 2: 0}
NCH = 5
CR = 80
DEEP = 1024


def kernel(
    t_in, b_in, l_in, r_in, out,
    tbuf, tp, rb, bbuf, bm, b0, lhs, lk, xs, acc0, accm, perm,
    give, swap, own_half, work, land, up_s, up_r, dn_s, dn_r, part, parts, rk, pz, pzs, py, pys, px,
    t_send, t_recv, f_send, f_recv, b_sem, r_sem,
    c_sem, d_sem, up_sem, dn_sem, s_sem, z_sem, y_sem, x_sem,
):
    x, yl, z, yh, c = (lax.axis_index(a) for a in AXES)
    me = {"x": x, "yl": yl, "z": z, "yh": yh, "c": c}

    def at(**over):
        return tuple(over.get(a, me[a]) for a in AXES)

    def near(dx, dy):
        return at(x=lax.rem(x + dx, 4), yh=lax.rem(yh + dy, 2))

    def to_z(k):
        return at(z=lax.rem(z + k, 8))

    def to_yc(k):
        v = lax.rem(yl * 4 + yh * 2 + c + k, 8)
        return at(yl=v // 4, yh=lax.rem(v // 2, 2), c=lax.rem(v, 2))

    def to_x(k):
        return at(x=lax.rem(x + k, 4))

    partner = at(c=1 - c)
    barrier = pltpu.get_barrier_semaphore()

    def greet(device):
        pl.semaphore_signal(barrier, inc=1, device_id=device, device_id_type=MESH)

    t_copy = pltpu.make_async_copy(t_in, tbuf, b_sem.at[3])
    t_copy.start()
    b_copies = [pltpu.make_async_copy(b_in.at[k], bbuf.at[k], b_sem.at[k]) for k in range(3)]
    for k in KINDS:
        b_copies[k].start()

    peers = [(dx, dy) for dx in range(4) for dy in range(2) if (dx, dy) != (0, 0)]
    for k in range(1, 8):
        greet(to_z(k))
    for dx, dy in peers:
        greet(near(dx, dy))
    for k in range(1, 8):
        greet(to_yc(k))
    own_role = yh * 2 + c
    for sl in range(2):
        for sh in range(2):
            same = (own_role == x) & (yl == c) & (sl == yl) & (sh == yh)

            @pl.when(jnp.logical_not(same))
            def _():
                greet(at(x=own_role, yl=sl, yh=sh, c=yl))

    def is_self(q, d):
        return (d * 2 + q == x) & (c == yl) & (x // 2 == yh) & (lax.rem(x, 2) == c)

    n_self = 0
    for q in range(2):
        for d in range(2):
            n_self = n_self + jnp.where(is_self(q, d), 1, 0)

    p = lax.broadcasted_iota(jnp.int32, (80, 80), 0)
    q_ = lax.broadcasted_iota(jnp.int32, (80, 80), 1)
    jj = (p * 3277) >> 16
    rest = p - jj * 20
    cc = (rest * 13108) >> 16
    group = jnp.where(cc * 20 + jj * 5 + (rest - cc * 5) == q_, 1.0, 0.0).astype(BF)
    lane80 = lax.broadcasted_iota(jnp.int32, (80, 128), 1)
    tail = jnp.zeros((80, 48), F32)

    def turned(block, s):
        block = jnp.concatenate([block.astype(F32), tail], axis=1)
        return block if s == 0 else pltpu.roll(block, (0, 80, 32)[s], 1)

    t_copy.wait()
    def top(kk):
        return tbuf[KINDS[kk // 20], kk % 20]

    for j in range(20):
        mid = turned(top(3 * j + 1), 1)
        packed = jnp.concatenate(
            [
                jnp.where(lane80 < 80, turned(top(3 * j), 0), mid).astype(BF),
                jnp.where(lane80 < 32, mid, turned(top(3 * j + 2), 2)).astype(BF),
            ],
            axis=1,
        )
        moved = jnp.dot(group, packed, preferred_element_type=F32).astype(BF)
        for to in range(4):
            tp[to, j * ROWS : (j + 1) * ROWS, :] = moved[to * ROWS : (to + 1) * ROWS, :]
    p = lax.broadcasted_iota(jnp.int32, (320, 320), 0)
    q_ = lax.broadcasted_iota(jnp.int32, (320, 320), 1)
    g_ = (p * 1639) >> 16
    rest = p - g_ * 40
    perm[...] = jnp.where((rest & 7) * 40 + g_ * 5 + (rest >> 3) == q_, 1.0, 0.0).astype(BF)
    for j in range(20):
        bm[j * 256 + 240 : j * 256 + 256, :] = jnp.zeros((16, 640), BF)
    for j in range(7):
        r = 240 if j < 6 else 160
        b0[j * 256 + r : j * 256 + 256, :] = jnp.zeros((256 - r, 640), BF)
    pl.semaphore_wait(barrier, 25 - n_self)

    def rows_of(n):
        return pl.ds(n * CR, CR)

    def piece(n, dx, dy):
        i = dx * 2 + dy
        src = tp.at[lax.rem(x + dx, 4), rows_of(n), :]
        dst = rb.at[yh * 2 + c, x, rows_of(n), :]
        if (dx, dy) == (0, 0):
            return pltpu.make_async_copy(src, dst, t_recv.at[n, i])
        return pltpu.make_async_remote_copy(
            src, dst, t_send.at[n, i], t_recv.at[n, i], device_id=near(dx, dy), device_id_type=MESH
        )

    order = [(0, 1), (1, 0), (3, 0), (1, 1), (3, 1), (2, 0), (2, 1), (0, 0)]
    for n in range(NCH):
        for dx, dy in order:
            piece(n, dx, dy).start()

    d_here = x // 2
    r_copies = []
    for t in range(5):
        for i, (src, dst, n) in enumerate(
            ((0, d_here * 128, 256), (256, 256 - d_here * 192, 64), (256, 320 - d_here * 320, 64))
        ):
            cp = pltpu.make_async_copy(
                r_in.at[t, pl.ds(src, n), :],
                rk.at[t, pl.ds(pl.multiple_of(dst, 64), n), :],
                r_sem.at[t * 3 + i],
            )
            cp.start()
            r_copies.append(cp)

    for a in range(8):
        row = l_in[a]
        for xx in range(4):
            block = row[:, xx * 80 : xx * 80 + 80]
            for s in range(3):
                lk[s, a * 128 : a * 128 + 80, xx * 128 : xx * 128 + 128] = turned(block, s).astype(BF)
        for s in range(3):
            lk[s, a * 128 + 80 : a * 128 + 128, :] = jnp.zeros((48, 512), BF)
    def bottoms(kind):
        b_copies[kind].wait()

        def row_of(kk):
            return pl.ds(pl.multiple_of((kk // 3) * 256 + lax.rem(kk, 3) * 80, 16), 80)

        def turn(k, carry):
            w = jnp.swapaxes(bbuf[kind, k], 0, 1)
            cat = jnp.concatenate([w[0], w[1][:, 256:320], w[1][:, 0:256]], axis=1)
            if kind == 0:
                b0[row_of(k), :] = cat
            bm[row_of(k + 20 * PARTNER[kind]), :] = cat * 2 if kind == 1 else cat
            return carry

        lax.fori_loop(0, 20, turn, 0)

    def forward(n, dy):
        ref = rb.at[dy * 2 + c, :, rows_of(n), :]
        return pltpu.make_async_remote_copy(
            ref, ref, f_send.at[n, dy], f_recv.at[n, dy], device_id=partner, device_id_type=MESH
        )

    def arrive(n):
        for dx in range(4):
            for dy in range(2):
                cp = piece(n, dx, dy)
                if (dx, dy) == (0, 0):
                    cp.wait()
                else:
                    cp.wait_recv()
        for dy in range(2):
            forward(n, dy).start()

    low = lax.broadcasted_iota(jnp.int32, (ROWS, 128), 1) < 64

    def expand(n):
        for dy in range(2):
            forward(n, dy).wait_recv()
        for j in range(4):
            src = slice((n * 4 + j) * ROWS, (n * 4 + j + 1) * ROWS)
            for h in range(4):
                rows = slice(j * 80 + h * ROWS, j * 80 + (h + 1) * ROWS)
                for xx in range(4):
                    t0 = rb[h, xx, src, 0:128]
                    t1 = rb[h, xx, src, 128:256]
                    cols = slice(xx * 128, xx * 128 + 128)
                    lhs[0, rows, cols] = t0
                    lhs[1, rows, cols] = jnp.where(low, t1, t0)
                    lhs[2, rows, cols] = t1
        xv = []
        for s in range(3):
            xv.append(
                lax.dot_general(lhs[s], lk[s], (((1,), (1,)), ((), ())), preferred_element_type=F32)
            )
        for j in range(4):
            for a in range(8):
                box = (slice(j * 80, j * 80 + 80), slice(a * 128, a * 128 + 128))
                mid = pltpu.roll(xv[1][box], 80, 1)
                last = pltpu.roll(xv[2][box], 32, 1)
                rows = slice(a * 80, a * 80 + 80)
                xs[rows, j * 256 : j * 256 + 128] = jnp.where(lane80 < 80, xv[0][box], mid).astype(BF)
                xs[rows, j * 256 + 128 : j * 256 + 256] = jnp.where(lane80 < 32, mid, last).astype(BF)

    def mixed(n):
        return jnp.dot(xs[...], bm[n * DEEP : (n + 1) * DEEP, :], preferred_element_type=F32)

    def half_of(a, g):
        return pl.ds(pl.multiple_of(a * 80 + g * 40, 8), 40)

    def swap_copy(q):
        return pltpu.make_async_remote_copy(
            give.at[q], swap.at[q], c_sem.at[0, q], c_sem.at[1, q],
            device_id=partner, device_id_type=MESH,
        )

    def share(q, acc):
        for a in range(8):
            give[q, a] = acc[half_of(a, 1 - c), :].astype(BF)
        swap_copy(q).start()

    def shared(q, acc):
        swap_copy(q).wait_recv()
        for a in range(8):
            own_half[a * 40 : a * 40 + 40, :] = (
                acc[half_of(a, c), :] + swap[q, a].astype(F32)
            ).astype(BF)
        moved = jnp.dot(perm[...], own_half[...], preferred_element_type=F32)
        work[q] = moved.reshape(8, 40, 640).astype(BF)

    def direct(k):
        return pltpu.make_async_remote_copy(
            work.at[0, lax.rem(z + k, 8)], land.at[k], d_sem.at[0, k], d_sem.at[1, k],
            device_id=to_z(k), device_id_type=MESH,
        )

    parts_of = ((0, 24), (24, 16))

    def up(g, s):
        rows = pl.ds(*parts_of[g])
        return pltpu.make_async_remote_copy(
            up_s.at[s, rows], up_r.at[s, rows], up_sem.at[0, g, s], up_sem.at[1, g, s],
            device_id=to_z(1), device_id_type=MESH,
        )

    def dn(g, s):
        rows = pl.ds(*parts_of[g])
        return pltpu.make_async_remote_copy(
            dn_s.at[s, rows], dn_r.at[s, rows], dn_sem.at[0, g, s], dn_sem.at[1, g, s],
            device_id=to_z(7), device_id_type=MESH,
        )

    slot = yl * 2 + yh

    def scatter(q, d):
        return pltpu.make_async_remote_copy(
            part.at[q, d], parts.at[slot], s_sem.at[0, q * 2 + d], s_sem.at[1, slot],
            device_id=(d * 2 + q, c, z, x // 2, lax.rem(x, 2)), device_id_type=MESH,
        )

    def hand_on(q, total):
        for d in range(2):
            part[q, d] = total[:, d * 256 : d * 256 + 384].astype(BF)

            @pl.when(jnp.logical_not(is_self(q, d)))
            def _():
                scatter(q, d).start()

            @pl.when(is_self(q, d))
            def _():
                pltpu.make_async_copy(part.at[q, d], parts.at[slot], s_sem.at[1, slot]).start()

    def gathered():
        for k in range(1, 8):
            direct(k).wait_recv()
        total = work[0, z].astype(F32)
        for k in range(1, 8):
            total = total + land[k].astype(F32)
        hand_on(0, total)

    def ring():
        for s in range(4):
            for g in range(2):
                rows = pl.ds(*parts_of[g])
                mine = work[1, lax.rem(z + 4 + s, 8), rows]
                if s > 0:
                    dn(g, s - 1).wait_recv()
                    mine = (mine.astype(F32) + dn_r[s - 1, rows].astype(F32)).astype(BF)
                dn_s[s, rows] = mine
                dn(g, s).start()
                if s < 3:
                    mine = work[1, lax.rem(z + 3 - s, 8), rows]
                    if s > 0:
                        up(g, s - 1).wait_recv()
                        mine = (mine.astype(F32) + up_r[s - 1, rows].astype(F32)).astype(BF)
                    up_s[s, rows] = mine
                    up(g, s).start()
        for g in range(2):
            up(g, 2).wait_recv()
            dn(g, 3).wait_recv()
        hand_on(1, work[1, z].astype(F32) + up_r[2].astype(F32) + dn_r[3].astype(F32))

    bottoms(0)
    bottoms(2)
    arrive(0)
    bottoms(1)
    expand(0)
    arrive(1)
    acc0[...] = jnp.dot(xs[...], b0[0:DEEP, :], preferred_element_type=F32)
    accm[...] = mixed(0)
    expand(1)
    arrive(2)
    acc0[...] += jnp.dot(xs[:, 0:768], b0[DEEP:1792, :], preferred_element_type=F32)
    share(0, acc0)
    accm[...] += mixed(1)
    shared(0, acc0)
    for k in (4, 3, 5, 2, 6, 1, 7):
        direct(k).start()
    expand(2)
    arrive(3)
    accm[...] += mixed(2)
    expand(3)
    arrive(4)
    accm[...] += mixed(3)
    expand(4)
    accm[...] += mixed(4)
    share(1, accm)
    gathered()
    shared(1, accm)
    ring()

    for i in range(4):
        pltpu.make_async_copy(part.at[0, 0], parts.at[i], s_sem.at[1, i]).wait()
    whole = (
        parts[0].astype(F32) + parts[1].astype(F32) + parts[2].astype(F32) + parts[3].astype(F32)
    )
    lanes = lax.broadcasted_iota(jnp.int32, (40, 384), 1) + d_here * 1024
    whole = jnp.where((lanes < 320) | (lanes >= 1088), whole, 0.0)
    for cp in r_copies:
        cp.wait()
    total = jnp.zeros((8, 320), F32)
    for t in range(5):
        total += jnp.dot(
            whole[t * 8 : t * 8 + 8, :].astype(BF), rk[t], preferred_element_type=F32
        )
    pzs[...] = total.astype(BF)

    def all_sum(src, land, sem, n, dest):
        copies = []
        for k in range(1, n):
            cp = pltpu.make_async_remote_copy(
                src, land.at[k], sem.at[0, k], sem.at[1, k], device_id=dest(k), device_id_type=MESH
            )
            cp.start()
            copies.append(cp)
        for cp in copies:
            cp.wait()
        s = src[...].astype(F32)
        for k in range(1, n):
            s = s + land[k].astype(F32)
        return s

    pys[...] = all_sum(pzs, pz, z_sem, 8, to_z)
    own = all_sum(pys, py, y_sem, 8, to_yc)
    px[x] = own * jnp.where(lax.rem(x, 2) == 0, 1.0, 0.25)
    copies = []
    for k in range(1, 4):
        cp = pltpu.make_async_remote_copy(
            px.at[x], px.at[x], x_sem.at[0, k], x_sem.at[1, k], device_id=to_x(k), device_id_type=MESH
        )
        cp.start()
        copies.append(cp)
    for cp in copies:
        cp.wait()
    for i in range(4):
        out[i % 2, i // 2] = px[i]

    for n in range(NCH):
        for dx, dy in peers:
            piece(n, dx, dy).wait_send()
        for dy in range(2):
            forward(n, dy).wait_send()
    for k in range(1, 8):
        direct(k).wait_send()
    for q in range(2):
        swap_copy(q).wait_send()
        for s in range(4):
            dn(q, s).wait_send()
            if s < 3:
                up(q, s).wait_send()
        for d in range(2):
            @pl.when(jnp.logical_not(is_self(q, d)))
            def _():
                scatter(q, d).wait_send()


def on_device(tops, bottoms, left_iso, right_iso):
    any_space = pl.BlockSpec(memory_space=pl.ANY)
    vmem_space = pl.BlockSpec(memory_space=VM)
    return pl.pallas_call(
        kernel,
        out_shape=jax.ShapeDtypeStruct((2, 2, 8, 320), F32),
        in_specs=[any_space, any_space, vmem_space, any_space],
        out_specs=vmem_space,
        scratch_shapes=[
            VM((3, 20, 80, 80), BF),
            VM((4, 400, 256), BF),
            VM((4, 4, 400, 256), BF),
            VM((3, 20, 80, 2, 320), BF),
            VM((5120, 640), BF),
            VM((1792, 640), BF),
            VM((3, 320, 512), BF),
            VM((3, 1024, 512), BF),
            VM((640, DEEP), BF),
            VM((640, 640), F32),
            VM((640, 640), F32),
            VM((320, 320), BF),
            VM((2, 8, 40, 640), BF),
            VM((2, 8, 40, 640), BF),
            VM((320, 640), BF),
            VM((2, 8, 40, 640), BF),
            VM((8, 40, 640), BF),
            VM((3, 40, 640), BF),
            VM((3, 40, 640), BF),
            VM((4, 40, 640), BF),
            VM((4, 40, 640), BF),
            VM((2, 2, 40, 384), BF),
            VM((4, 40, 384), BF),
            VM((5, 384, 320), BF),
            VM((8, 8, 320), BF),
            VM((8, 320), BF),
            VM((8, 8, 320), F32),
            VM((8, 320), F32),
            VM((4, 8, 320), F32),
            DMA((NCH, 8)),
            DMA((NCH, 8)),
            DMA((NCH, 2)),
            DMA((NCH, 2)),
            DMA((4,)),
            DMA((15,)),
            DMA((2, 2)),
            DMA((2, 8)),
            DMA((2, 2, 3)),
            DMA((2, 2, 4)),
            DMA((2, 4)),
            DMA((2, 8)),
            DMA((2, 8)),
            DMA((2, 4)),
        ],
        compiler_params=pltpu.CompilerParams(
            collective_id=0, has_side_effects=True, vmem_limit_bytes=60 << 20
        ),
    )(tops, bottoms, jnp.transpose(left_iso, (1, 2, 0)), right_iso)


def solution(mesh):
    torus = Mesh(mesh.devices.reshape(4, 2, 8, 2, 2), AXES)
    in_specs = (
        P(None, ("yl", "z"), ("yh", "c"), "x"),
        P(None, ("yl", "z"), ("yh", "c"), None, None),
        P(None, None, ("yh", "c")),
        P(("yl", "z", "yh", "c"), None, None),
    )
    return jax.shard_map(on_device, mesh=torus, in_specs=in_specs, out_specs=P(), check_vma=False)
```

```python
import jax
import jax.numpy as jnp
from jax import lax
from jax.experimental import pallas as pl
from jax.experimental.pallas import tpu as pltpu
from jax.sharding import Mesh
from jax.sharding import PartitionSpec as P

MESH = pl.DeviceIdType.MESH
AXES = ("x", "yl", "z", "yh", "c")
BF = jnp.bfloat16
F32 = jnp.float32
VM = pltpu.VMEM
DMA = pltpu.SemaphoreType.DMA

ROWS = 20
KINDS = (0, 2, 1)
PARTNER = {0: 1, 1: 2, 2: 0}
CHUNKS = ((0, 4), (4, 4), (8, 4), (12, 4), (16, 4))
NCH = len(CHUNKS)
DEEP = 1024


def kernel(
    t_in, b_in, l_in, r_in, out,
    tbuf, tp, rb, bbuf, bm, b0, lhs, lk, xs, acc0, accm, perm,
    give, swap, own_half, work, land, up_s, up_r, dn_s, dn_r, part, parts, rk, pz, pzs, py, pys, px,
    t_send, t_recv, f_send, f_recv, b_sem, r_sem,
    c_sem, d_sem, up_sem, dn_sem, s_sem, z_sem, y_sem, x_sem,
):
    x, yl, z, yh, c = (lax.axis_index(a) for a in AXES)
    me = {"x": x, "yl": yl, "z": z, "yh": yh, "c": c}

    def at(**over):
        return tuple(over.get(a, me[a]) for a in AXES)

    def near(dx, dy):
        return at(x=lax.rem(x + dx, 4), yh=lax.rem(yh + dy, 2))

    def to_z(k):
        return at(z=lax.rem(z + k, 8))

    def to_yc(k):
        v = lax.rem(yl * 4 + yh * 2 + c + k, 8)
        return at(yl=v // 4, yh=lax.rem(v // 2, 2), c=lax.rem(v, 2))

    def to_x(k):
        return at(x=lax.rem(x + k, 4))

    partner = at(c=1 - c)
    barrier = pltpu.get_barrier_semaphore()

    def greet(device):
        pl.semaphore_signal(barrier, inc=1, device_id=device, device_id_type=MESH)

    t_copy = pltpu.make_async_copy(t_in, tbuf, b_sem.at[3])
    t_copy.start()
    b_copies = [pltpu.make_async_copy(b_in.at[k], bbuf.at[k], b_sem.at[k]) for k in range(3)]
    for k in KINDS:
        b_copies[k].start()

    peers = [(dx, dy) for dx in range(4) for dy in range(2) if (dx, dy) != (0, 0)]
    for k in range(1, 8):
        greet(to_z(k))
    for dx, dy in peers:
        greet(near(dx, dy))
    for k in range(1, 8):
        greet(to_yc(k))
    own_role = yh * 2 + c
    for sl in range(2):
        for sh in range(2):
            same = (own_role == x) & (yl == c) & (sl == yl) & (sh == yh)

            @pl.when(jnp.logical_not(same))
            def _():
                greet(at(x=own_role, yl=sl, yh=sh, c=yl))

    def is_self(q, d):
        return (d * 2 + q == x) & (c == yl) & (x // 2 == yh) & (lax.rem(x, 2) == c)

    n_self = 0
    for q in range(2):
        for d in range(2):
            n_self = n_self + jnp.where(is_self(q, d), 1, 0)

    p = lax.broadcasted_iota(jnp.int32, (80, 80), 0)
    q_ = lax.broadcasted_iota(jnp.int32, (80, 80), 1)
    jj = (p * 3277) >> 16
    rest = p - jj * 20
    cc = (rest * 13108) >> 16
    group = jnp.where(cc * 20 + jj * 5 + (rest - cc * 5) == q_, 1.0, 0.0).astype(BF)
    lane80 = lax.broadcasted_iota(jnp.int32, (80, 128), 1)
    tail = jnp.zeros((80, 48), F32)

    def turned(block, s):
        block = jnp.concatenate([block.astype(F32), tail], axis=1)
        return block if s == 0 else pltpu.roll(block, (0, 80, 32)[s], 1)

    t_copy.wait()
    def top(kk):
        return tbuf[KINDS[kk // 20], kk % 20]

    for j in range(20):
        mid = turned(top(3 * j + 1), 1)
        packed = jnp.concatenate(
            [
                jnp.where(lane80 < 80, turned(top(3 * j), 0), mid).astype(BF),
                jnp.where(lane80 < 32, mid, turned(top(3 * j + 2), 2)).astype(BF),
            ],
            axis=1,
        )
        moved = jnp.dot(group, packed, preferred_element_type=F32).astype(BF)
        for to in range(4):
            tp[to, j * ROWS : (j + 1) * ROWS, :] = moved[to * ROWS : (to + 1) * ROWS, :]
    p = lax.broadcasted_iota(jnp.int32, (320, 320), 0)
    q_ = lax.broadcasted_iota(jnp.int32, (320, 320), 1)
    g_ = (p * 1639) >> 16
    rest = p - g_ * 40
    perm[...] = jnp.where((rest & 7) * 40 + g_ * 5 + (rest >> 3) == q_, 1.0, 0.0).astype(BF)
    for j in range(20):
        bm[j * 256 + 240 : j * 256 + 256, :] = jnp.zeros((16, 640), BF)
    for j in range(7):
        r = 240 if j < 6 else 160
        b0[j * 256 + r : j * 256 + 256, :] = jnp.zeros((256 - r, 640), BF)
    pl.semaphore_wait(barrier, 25 - n_self)

    def rows_of(n):
        return pl.ds(CHUNKS[n][0] * ROWS, CHUNKS[n][1] * ROWS)

    def piece(n, dx, dy):
        i = dx * 2 + dy
        src = tp.at[lax.rem(x + dx, 4), rows_of(n), :]
        dst = rb.at[yh * 2 + c, x, rows_of(n), :]
        if (dx, dy) == (0, 0):
            return pltpu.make_async_copy(src, dst, t_recv.at[n, i])
        return pltpu.make_async_remote_copy(
            src, dst, t_send.at[n, i], t_recv.at[n, i], device_id=near(dx, dy), device_id_type=MESH
        )

    order = [(0, 1), (1, 0), (3, 0), (1, 1), (3, 1), (2, 0), (2, 1), (0, 0)]
    for n in range(NCH):
        for dx, dy in order:
            piece(n, dx, dy).start()

    d_here = x // 2
    r_copies = []
    for t in range(5):
        for i, (src, dst, n) in enumerate(
            ((0, d_here * 128, 256), (256, 256 - d_here * 192, 64), (256, 320 - d_here * 320, 64))
        ):
            cp = pltpu.make_async_copy(
                r_in.at[t, pl.ds(src, n), :],
                rk.at[t, pl.ds(pl.multiple_of(dst, 64), n), :],
                r_sem.at[t * 3 + i],
            )
            cp.start()
            r_copies.append(cp)

    for a in range(8):
        row = l_in[a]
        for xx in range(4):
            block = row[:, xx * 80 : xx * 80 + 80]
            for s in range(3):
                lk[s, a * 128 : a * 128 + 80, xx * 128 : xx * 128 + 128] = turned(block, s).astype(BF)
        for s in range(3):
            lk[s, a * 128 + 80 : a * 128 + 128, :] = jnp.zeros((48, 512), BF)
    def bottoms(kind):
        b_copies[kind].wait()

        def row_of(kk):
            return pl.ds(pl.multiple_of((kk // 3) * 256 + lax.rem(kk, 3) * 80, 16), 80)

        def turn(k, carry):
            w = jnp.swapaxes(bbuf[kind, k], 0, 1)
            cat = jnp.concatenate([w[0], w[1][:, 256:320], w[1][:, 0:256]], axis=1)
            if kind == 0:
                b0[row_of(k), :] = cat
            bm[row_of(k + 20 * PARTNER[kind]), :] = cat * 2 if kind == 1 else cat
            return carry

        lax.fori_loop(0, 20, turn, 0)

    def forward(n, dy):
        ref = rb.at[dy * 2 + c, :, rows_of(n), :]
        return pltpu.make_async_remote_copy(
            ref, ref, f_send.at[n, dy], f_recv.at[n, dy], device_id=partner, device_id_type=MESH
        )

    def arrive(n):
        for dx in range(4):
            for dy in range(2):
                cp = piece(n, dx, dy)
                if (dx, dy) == (0, 0):
                    cp.wait()
                else:
                    cp.wait_recv()
        for dy in range(2):
            forward(n, dy).start()

    low = lax.broadcasted_iota(jnp.int32, (ROWS, 128), 1) < 64

    def expand(n):
        for dy in range(2):
            forward(n, dy).wait_recv()
        first, count = CHUNKS[n]
        for j in range(count):
            src = slice((first + j) * ROWS, (first + j + 1) * ROWS)
            for h in range(4):
                rows = slice(j * 80 + h * ROWS, j * 80 + (h + 1) * ROWS)
                for xx in range(4):
                    t0 = rb[h, xx, src, 0:128]
                    t1 = rb[h, xx, src, 128:256]
                    cols = slice(xx * 128, xx * 128 + 128)
                    lhs[0, rows, cols] = t0
                    lhs[1, rows, cols] = jnp.where(low, t1, t0)
                    lhs[2, rows, cols] = t1
        xv = []
        for s in range(3):
            xv.append(
                lax.dot_general(
                    lhs[s, 0 : count * 80, :], lk[s], (((1,), (1,)), ((), ())),
                    preferred_element_type=F32,
                )
            )
        for j in range(count):
            for a in range(8):
                box = (slice(j * 80, j * 80 + 80), slice(a * 128, a * 128 + 128))
                mid = pltpu.roll(xv[1][box], 80, 1)
                last = pltpu.roll(xv[2][box], 32, 1)
                rows = slice(a * 80, a * 80 + 80)
                xs[rows, j * 256 : j * 256 + 128] = jnp.where(lane80 < 80, xv[0][box], mid).astype(BF)
                xs[rows, j * 256 + 128 : j * 256 + 256] = jnp.where(lane80 < 32, mid, last).astype(BF)

    def mixed(n):
        first, count = CHUNKS[n]
        return jnp.dot(
            xs[:, 0 : count * 256], bm[first * 256 : (first + count) * 256, :],
            preferred_element_type=F32,
        )

    def half_of(a, g):
        return pl.ds(pl.multiple_of(a * 80 + g * 40, 8), 40)

    def swap_copy(q):
        return pltpu.make_async_remote_copy(
            give.at[q], swap.at[q], c_sem.at[0, q], c_sem.at[1, q],
            device_id=partner, device_id_type=MESH,
        )

    def share(q, acc):
        for a in range(8):
            give[q, a] = acc[half_of(a, 1 - c), :].astype(BF)
        swap_copy(q).start()

    def shared(q, acc):
        swap_copy(q).wait_recv()
        for a in range(8):
            own_half[a * 40 : a * 40 + 40, :] = (
                acc[half_of(a, c), :] + swap[q, a].astype(F32)
            ).astype(BF)
        moved = jnp.dot(perm[...], own_half[...], preferred_element_type=F32)
        work[q] = moved.reshape(8, 40, 640).astype(BF)

    def direct(k):
        return pltpu.make_async_remote_copy(
            work.at[0, lax.rem(z + k, 8)], land.at[k], d_sem.at[0, k], d_sem.at[1, k],
            device_id=to_z(k), device_id_type=MESH,
        )

    parts_of = ((0, 24), (24, 16))

    def up(g, s):
        rows = pl.ds(*parts_of[g])
        return pltpu.make_async_remote_copy(
            up_s.at[s, rows], up_r.at[s, rows], up_sem.at[0, g, s], up_sem.at[1, g, s],
            device_id=to_z(1), device_id_type=MESH,
        )

    def dn(g, s):
        rows = pl.ds(*parts_of[g])
        return pltpu.make_async_remote_copy(
            dn_s.at[s, rows], dn_r.at[s, rows], dn_sem.at[0, g, s], dn_sem.at[1, g, s],
            device_id=to_z(7), device_id_type=MESH,
        )

    slot = yl * 2 + yh

    def scatter(q, d):
        return pltpu.make_async_remote_copy(
            part.at[q, d], parts.at[slot], s_sem.at[0, q * 2 + d], s_sem.at[1, slot],
            device_id=(d * 2 + q, c, z, x // 2, lax.rem(x, 2)), device_id_type=MESH,
        )

    def hand_on(q, total):
        for d in range(2):
            part[q, d] = total[:, d * 256 : d * 256 + 384].astype(BF)

            @pl.when(jnp.logical_not(is_self(q, d)))
            def _():
                scatter(q, d).start()

            @pl.when(is_self(q, d))
            def _():
                pltpu.make_async_copy(part.at[q, d], parts.at[slot], s_sem.at[1, slot]).start()

    def gathered():
        for k in range(1, 8):
            direct(k).wait_recv()
        total = work[0, z].astype(F32)
        for k in range(1, 8):
            total = total + land[k].astype(F32)
        hand_on(0, total)

    def steps(down, g):
        return 4 if down == (g == 0) else 3

    def hop(down, g, s):
        n = steps(down, g)
        if s >= n:
            return
        rows = pl.ds(*parts_of[g])
        send, kept, taken = (dn, dn_s, dn_r) if down else (up, up_s, up_r)
        mine = work[1, lax.rem(z + (8 - n + s if down else n - s), 8), rows]
        if s > 0:
            send(g, s - 1).wait_recv()
            mine = (mine.astype(F32) + taken[s - 1, rows].astype(F32)).astype(BF)
        kept[s, rows] = mine
        send(g, s).start()

    def ring():
        for s in range(4):
            hop(True, 0, s)
            hop(False, 1, s)
            hop(True, 1, s)
            hop(False, 0, s)
        pieces = []
        for g in range(2):
            nd, nu = steps(True, g), steps(False, g)
            dn(g, nd - 1).wait_recv()
            up(g, nu - 1).wait_recv()
            r0, n = parts_of[g]
            pieces.append(
                dn_r[nd - 1, r0 : r0 + n].astype(F32) + up_r[nu - 1, r0 : r0 + n].astype(F32)
            )
        hand_on(1, work[1, z].astype(F32) + jnp.concatenate(pieces, axis=0))

    bottoms(0)
    bottoms(2)
    arrive(0)
    bottoms(1)
    expand(0)
    arrive(1)
    acc0[...] = jnp.dot(xs[...], b0[0:DEEP, :], preferred_element_type=F32)
    accm[...] = mixed(0)
    expand(1)
    arrive(2)
    acc0[...] += jnp.dot(xs[:, 0:768], b0[DEEP:1792, :], preferred_element_type=F32)
    share(0, acc0)
    accm[...] += mixed(1)
    shared(0, acc0)
    for k in (4, 3, 5, 2, 6, 1, 7):
        direct(k).start()
    expand(2)
    arrive(3)
    accm[...] += mixed(2)
    expand(3)
    arrive(4)
    accm[...] += mixed(3)
    expand(4)
    accm[...] += mixed(4)
    share(1, accm)
    gathered()
    shared(1, accm)
    ring()

    for i in range(4):
        pltpu.make_async_copy(part.at[0, 0], parts.at[i], s_sem.at[1, i]).wait()
    whole = (
        parts[0].astype(F32) + parts[1].astype(F32) + parts[2].astype(F32) + parts[3].astype(F32)
    )
    lanes = lax.broadcasted_iota(jnp.int32, (40, 384), 1) + d_here * 1024
    whole = jnp.where((lanes < 320) | (lanes >= 1088), whole, 0.0)
    for cp in r_copies:
        cp.wait()
    total = jnp.zeros((8, 320), F32)
    for t in range(5):
        total += jnp.dot(
            whole[t * 8 : t * 8 + 8, :].astype(BF), rk[t], preferred_element_type=F32
        )
    pzs[...] = total.astype(BF)

    def all_sum(src, land, sem, n, dest):
        copies = []
        for k in range(1, n):
            cp = pltpu.make_async_remote_copy(
                src, land.at[k], sem.at[0, k], sem.at[1, k], device_id=dest(k), device_id_type=MESH
            )
            cp.start()
            copies.append(cp)
        for cp in copies:
            cp.wait()
        s = src[...].astype(F32)
        for k in range(1, n):
            s = s + land[k].astype(F32)
        return s

    pys[...] = all_sum(pzs, pz, z_sem, 8, to_z)
    own = all_sum(pys, py, y_sem, 8, to_yc)
    px[x] = own * jnp.where(lax.rem(x, 2) == 0, 1.0, 0.25)
    copies = []
    for k in range(1, 4):
        cp = pltpu.make_async_remote_copy(
            px.at[x], px.at[x], x_sem.at[0, k], x_sem.at[1, k], device_id=to_x(k), device_id_type=MESH
        )
        cp.start()
        copies.append(cp)
    for cp in copies:
        cp.wait()
    for i in range(4):
        out[i % 2, i // 2] = px[i]

    for n in range(NCH):
        for dx, dy in peers:
            piece(n, dx, dy).wait_send()
        for dy in range(2):
            forward(n, dy).wait_send()
    for k in range(1, 8):
        direct(k).wait_send()
    for q in range(2):
        swap_copy(q).wait_send()
        for s in range(steps(True, q)):
            dn(q, s).wait_send()
        for s in range(steps(False, q)):
            up(q, s).wait_send()
        for d in range(2):
            @pl.when(jnp.logical_not(is_self(q, d)))
            def _():
                scatter(q, d).wait_send()


def on_device(tops, bottoms, left_iso, right_iso):
    any_space = pl.BlockSpec(memory_space=pl.ANY)
    vmem_space = pl.BlockSpec(memory_space=VM)
    return pl.pallas_call(
        kernel,
        out_shape=jax.ShapeDtypeStruct((2, 2, 8, 320), F32),
        in_specs=[any_space, any_space, vmem_space, any_space],
        out_specs=vmem_space,
        scratch_shapes=[
            VM((3, 20, 80, 80), BF),
            VM((4, 400, 256), BF),
            VM((4, 4, 400, 256), BF),
            VM((3, 20, 80, 2, 320), BF),
            VM((5120, 640), BF),
            VM((1792, 640), BF),
            VM((3, 320, 512), BF),
            VM((3, 1024, 512), BF),
            VM((640, DEEP), BF),
            VM((640, 640), F32),
            VM((640, 640), F32),
            VM((320, 320), BF),
            VM((2, 8, 40, 640), BF),
            VM((2, 8, 40, 640), BF),
            VM((320, 640), BF),
            VM((2, 8, 40, 640), BF),
            VM((8, 40, 640), BF),
            VM((4, 40, 640), BF),
            VM((4, 40, 640), BF),
            VM((4, 40, 640), BF),
            VM((4, 40, 640), BF),
            VM((2, 2, 40, 384), BF),
            VM((4, 40, 384), BF),
            VM((5, 384, 320), BF),
            VM((8, 8, 320), BF),
            VM((8, 320), BF),
            VM((8, 8, 320), F32),
            VM((8, 320), F32),
            VM((4, 8, 320), F32),
            DMA((NCH, 8)),
            DMA((NCH, 8)),
            DMA((NCH, 2)),
            DMA((NCH, 2)),
            DMA((4,)),
            DMA((15,)),
            DMA((2, 2)),
            DMA((2, 8)),
            DMA((2, 2, 4)),
            DMA((2, 2, 4)),
            DMA((2, 4)),
            DMA((2, 8)),
            DMA((2, 8)),
            DMA((2, 4)),
        ],
        compiler_params=pltpu.CompilerParams(
            collective_id=0, has_side_effects=True, vmem_limit_bytes=60 << 20
        ),
    )(tops, bottoms, jnp.transpose(left_iso, (1, 2, 0)), right_iso)


def solution(mesh):
    torus = Mesh(mesh.devices.reshape(4, 2, 8, 2, 2), AXES)
    in_specs = (
        P(None, ("yl", "z"), ("yh", "c"), "x"),
        P(None, ("yl", "z"), ("yh", "c"), None, None),
        P(None, None, ("yh", "c")),
        P(("yl", "z", "yh", "c"), None, None),
    )
    return jax.shard_map(on_device, mesh=torus, in_specs=in_specs, out_specs=P(), check_vma=False)
```
